32 devices in a mesh: sec: 4 (over x, core), gy: 4 (over z), gz: 2 (over y).
Axes of the slice: x: 2, y: 2, z: 4, core: 2. Of those that a mesh axis runs over, the one named last changes fastest.
Arguments:
- velocity: float32 [4, 3, 64, 256, 896], P('sec', None, 'gz', 'gy'), may hold values from -6 to 6
- diffusion: float32 [64], P('gz'), may hold values from 0.05 to 0.24
- turbines: int32 [3, 8, 3], replicated, may hold values from 0 to 895, as said below
- fringe_start: int32 [3], replicated, may hold values from 0 to 768
Outputs:
- velocity_out: float32 [4, 3, 64, 256, 896], P('sec', None, 'gz', 'gy')
The draws below stay inside these ranges and needn't reach their ends.
Inputs may be any that keep to these rules, and one draw needn't show every extreme that they name: turbines[f, t] = (x0, y0, z0) with x0 < 896, y0 + 16 <= 256, z0 + 16 <= 64.
All inputs are finite; a program needn't handle non-finite values.
Results may differ from the reference program's by a relative error of at most 0.0003.
Values sent between devices are 32-bit elements; how exact they have to be, the bound alone decides.
A program may use at most 192 MiB of HBM per device.

```python
import math
import jax
import jax.numpy as jnp
from jax import lax

NX = 896
NY = 256
NZ = 64
FRINGE = 128
DISK = 16
NTURB = 8
STEPS = 1
SEC = 4
FARMS = 3


def draw_turbines(key, part):
    subkeys = jax.random.split(jax.random.fold_in(key, 7), 3)
    plane_pos = jax.random.randint(subkeys[0], (FARMS, NTURB), 0, NX)
    span_pos = jax.random.randint(subkeys[1], (FARMS, NTURB), 0, NY - DISK + 1)
    height_pos = jax.random.randint(subkeys[2], (FARMS, NTURB), 0, NZ - DISK + 1)
    return jnp.stack([plane_pos, span_pos, height_pos], axis=-1).astype(jnp.int32)


def block_scale(stream_key, shape, cuts, low, top_value):
    def one(axis_at, shards_of):
        heights = jax.random.uniform(jax.random.fold_in(jax.random.fold_in(stream_key, 6), axis_at), (shards_of,), jnp.float32, low / len(cuts), top_value / len(cuts))
        return jnp.repeat(jnp.exp(heights), shape[axis_at] // shards_of).reshape((-1,) + (1,) * (len(shape) - axis_at - 1))

    loudness = one(*cuts[0])
    for cut in cuts[1:]:
        loudness = loudness * one(*cut)
    return loudness


def gaussian(stream_key, dims, spread, bound, shards=(), kind=jnp.bfloat16):
    drawn = jax.random.normal(stream_key, dims, jnp.float32) * spread
    if len(shards) > 0:
        drawn = block_scale(stream_key, dims, shards, -0.22, 0.18) * drawn
    return jnp.clip(drawn, min=-bound, max=bound).astype(kind)


def setup_inputs(seed: int = 0) -> dict:
    streams_of = jax.random.split(jax.random.key(seed), 5)
    velocity = gaussian(streams_of[0], (SEC, 3, NZ, NY, NX), 1.0, 6.0, ((0, 4), (2, 2), (3, 4)), jnp.float32)
    diffusion = jnp.clip(jnp.exp(math.log(0.24) - 1.5686159 * jax.random.uniform(streams_of[1], (NZ,), jnp.float32) ** block_scale(streams_of[1], (NZ,), ((0, 2),), -0.2, 0.2)), 0.05, 0.24)
    turbines = draw_turbines(jax.random.fold_in(streams_of[4], 71), 0)
    fringe_start = jax.random.randint(streams_of[3], (FARMS,), 0, NX - FRINGE + 1).astype(jnp.int32)
    return dict(velocity=velocity, diffusion=diffusion, turbines=turbines, fringe_start=fringe_start)


time_step = 0.2
thrust_coef = 1.5


def spectral_slope(values, axis_pos, length):
    wavenum = jnp.fft.fftfreq(length) * (2.0 * jnp.pi)
    wavenum = jnp.where(jnp.arange(length) == length // 2, 0.0, wavenum)
    layout = [1] * values.ndim
    layout[axis_pos] = length
    factor = (1j * wavenum).reshape(layout)
    spectrum = jnp.fft.fft(values, axis=axis_pos)
    return jnp.real(jnp.fft.ifft(factor * spectrum, axis=axis_pos)).astype(values.dtype)


def reference(velocity, diffusion, turbines, fringe_start):
    current = velocity
    plane_index = jnp.arange(NX, dtype=jnp.int32)
    for step_index in range(STEPS):
        advanced_all = []
        for section in range(SEC):
            fields = current[section]
            updated = []
            for component in range(3):
                one_field = fields[component]
                along_x = spectral_slope(one_field, 2, NX)
                along_y = spectral_slope(one_field, 1, NY)
                advection = -((1.0 + fields[0]) * along_x + fields[1] * along_y)
                padded = jnp.pad(one_field, ((1, 1), (0, 0), (0, 0)))
                laplace = padded[2:] + padded[:-2] - 2.0 * one_field
                updated.append(one_field + time_step * advection + diffusion[:, None, None] * laplace)
            if section > 0:
                forcing = jnp.zeros_like(fields[0])
                for turbine in range(NTURB):
                    corner = turbines[section - 1, turbine].astype(jnp.int32)
                    anchor = (corner[2], corner[1], corner[0])
                    rotor = lax.dynamic_slice(fields[0], anchor, (DISK, DISK, 1))
                    speed = 1.0 + jnp.sum(rotor) / (DISK * DISK)
                    thrust = -0.5 * thrust_coef * speed * jnp.abs(speed)
                    patch = lax.dynamic_slice(forcing, anchor, (DISK, DISK, 1)) + thrust
                    forcing = lax.dynamic_update_slice(forcing, patch, anchor)
                updated[0] = updated[0] + time_step * forcing
            advanced_all.append(jnp.stack(updated))
        inflow = advanced_all[0][..., NX - FRINGE:]
        blended = [advanced_all[0]]
        for section in range(1, SEC):
            first_plane = fringe_start[section - 1].astype(jnp.int32)
            offset = plane_index - first_plane
            inside = (offset >= 0) & (offset < FRINGE)
            weight = jnp.where(inside, jnp.sin(jnp.pi * (offset.astype(jnp.float32) + 0.5) / FRINGE) ** 2, 0.0)
            placed = lax.dynamic_update_slice_in_dim(jnp.zeros_like(advanced_all[section]), inflow, first_plane, 3)
            blended.append(advanced_all[section] + weight * (placed - advanced_all[section]))
        current = jnp.stack(blended)
    return current
```

```python
import functools

import jax
import jax.numpy as jnp
import numpy as np
from jax import lax
from jax.experimental import pallas as pl
from jax.experimental.pallas import tpu as pltpu
from jax.sharding import PartitionSpec as P

FRINGE = 128
DISK = 16
LANES = 128
KEEP = 16

time_step = 0.2
thrust_coef = 1.5


def slope_matrix(n):
    i = np.arange(n)
    d = (i[:, None] - i[None, :]) % n
    safe = np.where(d == 0, 1, d)
    return np.where(d == 0, 0.0, np.pi / n * (1.0 - 2.0 * (d % 2)) / np.tan(safe * np.pi / n))


def leading(matrix, keep):
    basis = np.linalg.svd(matrix, full_matrices=False)[2][:keep].T
    signs = np.sign(basis[np.argmax(np.abs(basis), axis=0), np.arange(basis.shape[1])])
    return np.round(basis * signs * 2.0**25) / 2.0**25


def flow_factors(matrix, devices, keep):
    width = matrix.shape[0] // devices
    block = lambda a, b: matrix[a * width : (a + 1) * width, b * width : (b + 1) * width]
    keep = min(keep, width)
    basis = leading(np.concatenate([block(a, 0) for a in range(1, devices)], axis=0), keep)
    merges, applies = [], []
    for order in (list(range(devices)), list(range(devices))[::-1]):
        merge = np.zeros((devices, keep, 2 * keep))
        apply = np.zeros((devices, width, keep))
        before = None
        for at in range(devices - 1):
            sources, targets = order[: at + 1], order[at + 1 :]
            rows = np.concatenate([np.concatenate([block(a, b) @ basis for b in sources], axis=1) for a in targets], axis=0)
            held = leading(rows, keep)
            if before is not None:
                merge[order[at], :, :keep] = held[: at * keep].T @ before
            merge[order[at], :, keep:] = held[at * keep :].T
            apply[targets[0]] = rows[:width] @ held
            before = held
        merges.append(merge)
        applies.append(apply)
    return basis, merges[0], merges[1], np.concatenate(applies, axis=2)


def halves(x):
    x = np.asarray(x, np.float32)
    high = x.astype(jnp.bfloat16)
    return np.stack([high, (x - high.astype(np.float32)).astype(jnp.bfloat16)])


def split(x):
    high = x.astype(jnp.bfloat16)
    return high, (x - high.astype(jnp.float32)).astype(jnp.bfloat16)


def mm(a, b):
    return jnp.dot(a, b, preferred_element_type=jnp.float32)


def const_left(const_ref, data):
    high, low = split(data)
    return mm(const_ref[0], high) + mm(const_ref[0], low) + mm(const_ref[1], high)


def const_right(high, low, const_ref):
    return mm(high, const_ref[0]) + mm(low, const_ref[0]) + mm(high, const_ref[1])


def project_kernel(chunks, x_ref, basis_ref, out_ref):
    for i in range(x_ref.shape[0]):
        got = const_left(basis_ref, x_ref[i])
        for q in range(chunks):
            c = (q + chunks - 1) % chunks
            out_ref[q, i] = got[:, c * LANES : (c + 1) * LANES]


def merge_kernel(group, pos_ref, mr_ref, pr_ref, ml_ref, pleft_ref, wr_ref, wl_ref, outr_ref, outl_ref):
    for m_ref, p_ref, w_ref, out_ref in ((mr_ref, pr_ref, wr_ref, outr_ref), (ml_ref, pleft_ref, wl_ref, outl_ref)):
        for g in range(m_ref.shape[0] // group):
            ids = range(g * group, (g + 1) * group)
            data = jnp.concatenate(
                [jnp.concatenate([m_ref[i] for i in ids], axis=1), jnp.concatenate([p_ref[0, i] for i in ids], axis=1)], axis=0
            )
            got = const_left(w_ref, data)
            for at, i in enumerate(ids):
                out_ref[i] = got[:, at * LANES : (at + 1) * LANES]


def main_kernel(first, last_step, total, diff_ref, cur_ref, prev_ref, next_ref, low_ref, high_ref, mx_ref, my_ref, *rest):
    out_ref = rest[-1]
    step = first + pl.program_id(0)
    zb, width, length = cur_ref.shape[1:]
    for c in range(3):
        flat = cur_ref[c].reshape(zb * width, length)
        high, low = split(flat)
        along_x = const_right(high, low, mx_ref)
        for i in range(zb):
            here = cur_ref[c, i]
            hh, ll = high[i * width : (i + 1) * width], low[i * width : (i + 1) * width]
            along_y = mm(my_ref[0], hh) + mm(my_ref[0], ll) + mm(my_ref[1], hh)
            below = cur_ref[c, i - 1] if i > 0 else jnp.where(step == 0, low_ref[c], prev_ref[c, 0])
            above = cur_ref[c, i + 1] if i < zb - 1 else jnp.where(step == last_step, high_ref[c], next_ref[c, 0])
            tendency = (1.0 + cur_ref[0, i]) * along_x[i * width : (i + 1) * width] + cur_ref[1, i] * along_y
            laplace = above + below - 2.0 * here
            out_ref[c, i] = here - time_step * tendency + diff_ref[step * zb + i] * laplace


def far_kernel(chunk, devices, emit, ints_ref, thrust_ref, *refs):
    rights, lefts = refs[: devices - 1], refs[devices - 1 : 2 * devices - 2]
    ef_ref, v_ref, buf_ref = refs[2 * devices - 2 : 2 * devices + 1]
    out_ref = refs[2 * devices + 1]
    me = ints_ref[0]
    zb, width = v_ref.shape[1:3]

    def pick(arrays, at, c, i):
        got = arrays[-1][c, i]
        for j in range(devices - 2):
            got = jnp.where(at == j + 1, arrays[j][c, i], got)
        return got

    for c in range(3):
        for i in range(0, zb, 2):
            pair = []
            for j in (i, i + 1):
                pair.append(jnp.concatenate([pick(rights, me, c, j), pick(lefts, devices - 1 - me, c, j)], axis=0))
            got = const_left(ef_ref, jnp.concatenate(pair, axis=1))
            for at, j in enumerate((i, i + 1)):
                out_ref[c, j] = buf_ref[c, j] - time_step * (v_ref[0, j] * got[:, at * LANES : (at + 1) * LANES])

    y0, z0 = ints_ref[1], ints_ref[2] + pl.program_id(0) * zb
    for t in range((ints_ref.shape[0] - 3) // 3):
        tx, ty, tz = (ints_ref[3 + 3 * t + k] for k in range(3))

        @pl.when((tx // LANES == chunk) & (tz < z0 + zb) & (tz + DISK > z0) & (ty < y0 + width) & (ty + DISK > y0))
        def _():
            shape = (zb, width, LANES)
            zs = z0 + lax.broadcasted_iota(jnp.int32, shape, 0)
            ys = y0 + lax.broadcasted_iota(jnp.int32, shape, 1)
            xs = chunk * LANES + lax.broadcasted_iota(jnp.int32, shape, 2)
            hit = (xs == tx) & (ys >= ty) & (ys < ty + DISK) & (zs >= tz) & (zs < tz + DISK)
            out_ref[0] = out_ref[0] + jnp.where(hit, time_step * thrust_ref[t], 0.0)

    if emit:
        refs[-1][...] = out_ref[...]


def rotor_kernel(ints_ref, u_ref, out_ref):
    t = pl.program_id(0)
    tx, ty, tz = (ints_ref[3 + 3 * t + k] for k in range(3))
    shape = u_ref.shape[1:]
    zs = ints_ref[2] + lax.broadcasted_iota(jnp.int32, shape, 0)
    ys = ints_ref[1] + lax.broadcasted_iota(jnp.int32, shape, 1)
    xs = (tx // LANES) * LANES + lax.broadcasted_iota(jnp.int32, shape, 2)
    hit = (xs == tx) & (ys >= ty) & (ys < ty + DISK) & (zs >= tz) & (zs < tz + DISK)
    got = jnp.where(hit, u_ref[0], 0.0)
    folded = jnp.sum(jnp.sum(got, axis=0).reshape(-1, 8, LANES), axis=0)
    out_ref[0] = folded


def blend_kernel(ints_ref, buf_ref, inflow_ref, out_ref):
    start, farm, chunks = ints_ref[0], ints_ref[1], ints_ref[2]
    block = blend_block(pl.program_id(0), start, chunks)
    xs = block * LANES + lax.broadcasted_iota(jnp.int32, (1, LANES), 1)
    offset = xs - start
    inside = (offset >= 0) & (offset < FRINGE) & (farm > 0)
    weight = jnp.where(inside, jnp.sin(jnp.pi * (offset.astype(jnp.float32) + 0.5) / FRINGE) ** 2, 0.0)
    turn = lax.rem(start, LANES)
    for c in range(buf_ref.shape[0]):
        for i in range(buf_ref.shape[1]):
            here = buf_ref[c, i]
            out_ref[c, i] = here + weight * (pltpu.roll(inflow_ref[c, i], turn, 1) - here)


def blend_block(j, start, chunks):
    base = start // LANES
    after = jnp.where(base + 1 < chunks, base + 1, base - 1)
    return jnp.where(j == 0, base, after)


def params(kernel_grid=1):
    return pltpu.CompilerParams(dimension_semantics=("arbitrary",) * kernel_grid, vmem_limit_bytes=56 * 1024 * 1024)


def cost(flops, bytes_accessed):
    return pl.CostEstimate(flops=int(flops), bytes_accessed=int(bytes_accessed), transcendentals=0)


def whole(array):
    rank = len(array.shape)
    return pl.BlockSpec(array.shape, lambda *_: (0,) * rank)


def total_over(x, axis):
    size = lax.axis_size(axis)
    hop = 1
    while hop < size:
        x = x + lax.ppermute(x, axis, [(i, i ^ hop) for i in range(size)])
        hop *= 2
    return x


def body(velocity, diffusion, turbines, fringe_start):
    current = velocity[0]
    _, depth, width, length = current.shape
    devices = lax.axis_size("gy")
    rows = 3 * depth
    chunks = length // LANES
    me = lax.axis_index("gy")
    section = lax.axis_index("sec")
    f32 = jnp.float32

    basis, merge_r, merge_l, apply = flow_factors(slope_matrix(width * devices), devices, KEEP)
    keep = basis.shape[1]
    mx = jnp.asarray(halves(slope_matrix(length).T))
    my = jnp.asarray(halves(slope_matrix(width * devices)[:width, :width]))
    basis_c = jnp.asarray(halves(basis.T))
    mine = lambda m: lax.dynamic_index_in_dim(jnp.asarray(halves(m)), me, 1, keepdims=False)
    wr, wl, ef = mine(merge_r), mine(merge_l), mine(apply)

    farm_row = jnp.maximum(section - 1, 0)
    is_farm = (section > 0).astype(jnp.int32)
    corners = lax.dynamic_index_in_dim(turbines, farm_row, 0, keepdims=False)
    ints = jnp.concatenate(
        [jnp.stack([me, me * width, lax.axis_index("gz") * depth]).astype(jnp.int32), corners.reshape(-1)]
    )

    zg = 8
    coeffs = pl.pallas_call(
        functools.partial(project_kernel, chunks),
        out_shape=jax.ShapeDtypeStruct((chunks, rows, keep, LANES), f32),
        grid=(rows // zg,),
        in_specs=[pl.BlockSpec((zg, width, length), lambda i: (i, 0, 0)), whole(basis_c)],
        out_specs=pl.BlockSpec((chunks, zg, keep, LANES), lambda i: (0, i, 0, 0)),
        compiler_params=params(),
        cost_estimate=cost(6 * rows * keep * 256 * length, 4 * rows * length * (width + keep)),
        name="project",
    )(current.reshape(rows, width, length), basis_c)

    count = lax.axis_size("gz")
    up = [(i, i + 1) for i in range(count - 1)]
    down = [(i + 1, i) for i in range(count - 1)]
    low_halo = lax.ppermute(current[:, -1], "gz", up)
    high_halo = lax.ppermute(current[:, 0], "gz", down)

    turbine_count = corners.shape[0]
    sums = pl.pallas_call(
        rotor_kernel,
        out_shape=jax.ShapeDtypeStruct((turbine_count, 8, LANES), f32),
        grid_spec=pltpu.PrefetchScalarGridSpec(
            num_scalar_prefetch=1,
            grid=(turbine_count,),
            in_specs=[pl.BlockSpec((1, depth, width, LANES), lambda t, ints: (0, 0, 0, ints[3 + 3 * t] // LANES))],
            out_specs=pl.BlockSpec((1, 8, LANES), lambda t, ints: (t, 0, 0)),
        ),
        compiler_params=params(),
        cost_estimate=cost(1e6, turbine_count * depth * width * LANES * 4),
        name="rotor",
    )(ints, current)
    sums = jnp.sum(sums, axis=(1, 2))
    sums = total_over(total_over(sums, "gz"), "gy")
    speed = 1.0 + sums / (DISK * DISK)
    thrust = -0.5 * thrust_coef * speed * jnp.abs(speed) * is_farm.astype(f32)

    pieces = 4
    zb = 4 if depth % (4 * pieces) == 0 else 2
    steps = depth // zb
    per = steps // pieces

    def main_piece(p, buffer):
        at = lambda i: p * per + i
        in_specs = [
            pl.BlockSpec((3, zb, width, length), lambda i, d: (0, at(i), 0, 0)),
            pl.BlockSpec((3, 1, width, length), lambda i, d: (0, jnp.maximum(at(i) * zb - 1, 0), 0, 0)),
            pl.BlockSpec((3, 1, width, length), lambda i, d: (0, jnp.minimum(at(i) * zb + zb, depth - 1), 0, 0)),
            whole(low_halo), whole(high_halo), whole(mx), whole(my),
        ]
        args = [current, current, current, low_halo, high_halo, mx, my]
        aliases = {}
        if buffer is not None:
            in_specs.append(pl.BlockSpec(memory_space=pl.ANY))
            args.append(buffer)
            aliases = {len(args): 0}
        return pl.pallas_call(
            functools.partial(main_kernel, p * per, steps - 1, depth),
            out_shape=jax.ShapeDtypeStruct(current.shape, f32),
            grid_spec=pltpu.PrefetchScalarGridSpec(
                num_scalar_prefetch=1, grid=(per,), in_specs=in_specs,
                out_specs=pl.BlockSpec((3, zb, width, length), lambda i, d: (0, at(i), 0, 0)),
            ),
            input_output_aliases=aliases,
            compiler_params=params(),
            cost_estimate=cost(6 * rows * width * length * length // pieces, 10 * rows * width * length // pieces),
            name=f"main_{p}",
        )(diffusion, *args)

    def merge_step(t, from_left, from_right):
        position = jnp.clip(jnp.stack([t - me, t - (devices - 1 - me)]), 0, chunks - 1).astype(jnp.int32)
        part = rows // 2
        block = pl.BlockSpec((part, keep, LANES), lambda i, pos: (i, 0, 0))
        group = 8 if part % 8 == 0 else 2
        shape = jax.ShapeDtypeStruct((rows, keep, LANES), f32)
        return pl.pallas_call(
            functools.partial(merge_kernel, group),
            out_shape=(shape, shape),
            grid_spec=pltpu.PrefetchScalarGridSpec(
                num_scalar_prefetch=1,
                grid=(2,),
                in_specs=[
                    block, pl.BlockSpec((1, part, keep, LANES), lambda i, pos: (pos[0], i, 0, 0)),
                    block, pl.BlockSpec((1, part, keep, LANES), lambda i, pos: (pos[1], i, 0, 0)),
                    whole(wr), whole(wl),
                ],
                out_specs=(block, block),
            ),
            compiler_params=params(),
            cost_estimate=cost(12 * rows * keep * 256 * LANES, 24 * rows * keep * LANES),
            name="merge",
        )(position, from_left, coeffs, from_right, coeffs, wr, wl)

    z_far = min(16, depth)

    def far_chunk(q, rights, lefts, buffer):
        chunk = (q + chunks - 1) % chunks
        emit = q == 0
        block = pl.BlockSpec((3, z_far, keep, LANES), lambda i, *_: (0, i, 0, 0))
        wide = pl.BlockSpec((3, z_far, width, LANES), lambda i, *_: (0, i, 0, chunk))
        shapes = [jax.ShapeDtypeStruct(current.shape, f32)]
        outs = [wide]
        if emit:
            shapes.append(jax.ShapeDtypeStruct((3, depth, width, LANES), f32))
            outs.append(pl.BlockSpec((3, z_far, width, LANES), lambda i, *_: (0, i, 0, 0)))
        shaped = [x.reshape(3, depth, keep, LANES) for x in rights + lefts]
        return pl.pallas_call(
            functools.partial(far_kernel, chunk, devices, emit),
            out_shape=shapes,
            grid_spec=pltpu.PrefetchScalarGridSpec(
                num_scalar_prefetch=2,
                grid=(depth // z_far,),
                in_specs=[block] * len(shaped) + [
                    whole(ef), pl.BlockSpec((1, z_far, width, LANES), lambda i, *_: (1, i, 0, chunk)), wide,
                ],
                out_specs=outs,
            ),
            input_output_aliases={2 + len(shaped) + 2: 0},
            compiler_params=params(),
            cost_estimate=cost(6 * rows * width * 256 * LANES, 4 * rows * LANES * (3 * width + 6 * keep)),
            name=f"far_{q}",
        )(ints, thrust, *shaped, ef, current, buffer)

    rights, lefts = [], []
    zeros = jnp.zeros((rows, keep, LANES), f32)
    from_left, from_right = zeros, zeros
    buffer = None
    inflow = None
    done_pieces = 0
    for t in range(chunks + devices - 2):
        send_r, send_l = merge_step(t, from_left, from_right)
        live = [d for d in range(devices - 1) if 0 <= t - d < chunks]
        from_left = lax.ppermute(send_r, "gy", [(d, d + 1) for d in live])
        from_right = lax.ppermute(send_l, "gy", [(devices - 1 - d, devices - 2 - d) for d in live])
        rights.append(from_left)
        lefts.append(from_right)
        while done_pieces < pieces and (done_pieces < 2 * (t + 1)):
            buffer = main_piece(done_pieces, buffer)
            done_pieces += 1
        q = t - (devices - 2)
        if q >= 0:
            got = far_chunk(q, rights[q : q + devices - 1], lefts[q : q + devices - 1], buffer)
            buffer = got[0]
            if q == 0:
                sent = got[1]
                sections = lax.axis_size("sec")
                half = sections // 2
                near = lax.ppermute(sent, "sec", [(0, 1)])
                across = lax.ppermute(sent, "sec", [(0, half)])
                beyond = lax.ppermute(across, "sec", [(half, half + 1)])
                inflow = jnp.where(section == 1, near, jnp.where(section == half, across, beyond))

    start = lax.dynamic_index_in_dim(fringe_start, farm_row, 0, keepdims=False)
    blend_ints = jnp.stack([start, is_farm, jnp.int32(chunks)]).astype(jnp.int32)
    zc = min(8, depth)
    spot = pl.BlockSpec((3, zc, width, LANES), lambda j, i, ints: (0, i, 0, blend_block(j, ints[0], chunks)))
    out = pl.pallas_call(
        blend_kernel,
        out_shape=jax.ShapeDtypeStruct(current.shape, f32),
        grid_spec=pltpu.PrefetchScalarGridSpec(
            num_scalar_prefetch=1,
            grid=(2, depth // zc),
            in_specs=[spot, pl.BlockSpec((3, zc, width, LANES), lambda j, i, ints: (0, i, 0, 0))],
            out_specs=spot,
        ),
        input_output_aliases={1: 0},
        compiler_params=params(2),
        cost_estimate=cost(1e6, 24 * rows * width * LANES),
        name="blend",
    )(blend_ints, buffer, inflow)
    return out[None]


def solution(mesh):
    in_specs = (P("sec", None, "gz", "gy", None), P("gz"), P(), P())
    out_specs = P("sec", None, "gz", "gy", None)
    return jax.shard_map(body, mesh=mesh, in_specs=in_specs, out_specs=out_specs, check_vma=False)
```
